128 devices in a mesh: store: 8 (over z_lo, y), mod: 16 (over z_hi, x, core).
Axes of the slice: x: 4, y: 4, z: 4 (z_hi: 2, z_lo: 2; z = z_hi * 2 + z_lo), core: 2. Of those that a mesh axis runs over, the one named last changes fastest.
Arguments:
- act_proj: bfloat16 [1024, 256, 1024], P(('store', 'mod')), may hold values from -1.5 to 1.5
- grad_proj: bfloat16 [1024, 256, 1024], P(('store', 'mod')), may hold values from -1.5 to 1.5
- token_mask: int32 [1024, 256], P(('store', 'mod')), may hold values 0 or 1
- layer_of: int32 [32], P('mod'), may hold values from 0 to 3, as said below
- layer_weight: float32 [4], replicated, may hold values from 0.25 to 4
- fisher_inv: bfloat16 [32, 1024, 1024], P('mod'), may hold values from -0.2 to 1.8
- stored_grads: bfloat16 [32768, 32768], P('store', 'mod'), may hold values from -0.049804688 to 0.049804688
Outputs:
- scores: float32 [1024, 32768], P('mod', 'store')
The draws below stay inside these ranges and needn't reach their ends.
Inputs may be any that keep to these rules, and one draw needn't show every extreme that they name: `layer_of`: each of the 4 layers holds the same number of modules.
All inputs are finite; a program needn't handle non-finite values. No bound on the sum of `token_mask` on one device may be relied on, other than what follows from the above.
Results may differ from the reference program's by a relative error of at most 0.004.
Values may be sent and summed in bfloat16 or wider, within the bound.
No kernel may reach another device: no remote copies, remote signals or barrier semaphores. Data moves between devices by JAX's collectives and lax.ppermute only.
A program may use at most 128 MiB of HBM per device.

```python
import math
import jax
import jax.numpy as jnp
from jax import lax

R = 32
RR = 1024
LEN = 256
MODS = 32
LAYERS = 4
Q = 1024
NSTORE = 32768


def draw_layer_of(key, part):
    order = jax.random.permutation(key, jnp.arange(MODS, dtype=jnp.int32))
    return (order % LAYERS).astype(jnp.int32)


def draw_fisher_inv(key, part):
    key_off = jax.random.fold_in(key, 11)
    key_diag = jax.random.fold_in(key, 23)
    spread = 0.5 / math.sqrt(RR)
    off_part = jax.random.normal(key_off, (MODS, RR, RR), jnp.float32) * spread
    off_part = (off_part + jnp.swapaxes(off_part, 1, 2)) / math.sqrt(2.0)
    off_part = jnp.clip(off_part, -0.15, 0.15)
    diag_part = jax.random.uniform(key_diag, (MODS, RR), jnp.float32, 0.8, 1.6)
    ident = jnp.eye(RR, dtype=jnp.float32)
    return (off_part + diag_part[:, :, None] * ident[None, :, :]).astype(jnp.bfloat16)


def plant(drawn, own_key, smallest, top_value):
    extent = drawn.shape
    spot = [jax.random.randint(jax.random.fold_in(own_key, axis), (), 0, extent[axis]) for axis in range(len(extent))]
    drawn = drawn.at[tuple(spot)].set(smallest)
    longest = extent.index(max(extent))
    spot[longest] = (spot[longest] + 1) % extent[longest]
    return drawn.at[tuple(spot)].set(top_value)


def level_of(rng, extent, pieces, smallest, largest):
    factor_of = 1.0
    for axis_at, parts in pieces:
        steps = jax.random.uniform(jax.random.fold_in(jax.random.fold_in(rng, 6), axis_at), (parts,), jnp.float32, smallest / len(pieces), largest / len(pieces))
        factor_of = factor_of * jnp.repeat(jnp.exp(steps), extent[axis_at] // parts).reshape((-1,) + (1,) * (len(extent) - 1 - axis_at))
    return factor_of


def gaussian(stream_key, dims, scale, limit, shards=(), kind=jnp.bfloat16):
    loudness = level_of(stream_key, dims, shards, -0.22, 0.18) if shards else 1.0
    entries = jax.random.normal(stream_key, dims, jnp.float32) * scale * loudness
    return jnp.minimum(jnp.maximum(entries, -limit), limit).astype(kind)


def setup_inputs(seed: int = 0) -> dict:
    splits = jax.random.split(jax.random.key(seed), 8)
    act_proj = gaussian(splits[0], (Q, LEN, MODS * R), 0.25, 1.5, ((0, 128),))
    grad_proj = gaussian(splits[1], (Q, LEN, MODS * R), 0.25, 1.5, ((0, 128),))
    token_mask = plant((jax.random.randint(splits[2], (Q, LEN), 0, 4) < 3).astype(jnp.int32), jax.random.fold_in(splits[2], 1), 0, 1)
    layer_of = draw_layer_of(jax.random.fold_in(splits[7], 71), 0)
    layer_weight = jnp.clip(jnp.exp(jax.random.uniform(splits[4], (LAYERS,), jnp.float32, math.log(0.25), math.log(4.0))), 0.25, 4.0)
    fisher_inv = draw_fisher_inv(jax.random.fold_in(splits[7], 71), 0)
    stored_grads = gaussian(splits[6], (NSTORE, MODS * RR), 0.0078125, 0.049804688, ((0, 8), (1, 16)))
    return dict(act_proj=act_proj, grad_proj=grad_proj, token_mask=token_mask, layer_of=layer_of, layer_weight=layer_weight, fisher_inv=fisher_inv, stored_grads=stored_grads)


def reference(act_proj, grad_proj, token_mask, layer_of, layer_weight, fisher_inv, stored_grads):
    valid_mask = token_mask.astype(jnp.bfloat16)[:, :, None]
    grad_side = (grad_proj * valid_mask).reshape(Q, LEN, MODS, R)
    act_side = act_proj.reshape(Q, LEN, MODS, R)

    def one_query(pair):
        grad_one, act_one = pair
        outer = jnp.einsum("tmi,tmj->mij", grad_one.astype(jnp.float32), act_one.astype(jnp.float32))
        return outer.reshape(MODS, R * R)

    per_sample = lax.map(one_query, (grad_side, act_side)).astype(jnp.bfloat16)
    picked = layer_of[:, None] == jnp.arange(LAYERS, dtype=jnp.int32)[None, :]
    module_weight = jnp.sum(jnp.where(picked, layer_weight[None, :], jnp.zeros_like(layer_weight)[None, :]), axis=1)
    conditioned = jnp.einsum("qkr,krc->qkc", per_sample.astype(jnp.float32), fisher_inv.astype(jnp.float32))
    conditioned = (conditioned * module_weight[None, :, None]).astype(jnp.bfloat16)
    return jnp.dot(conditioned.reshape(Q, MODS * RR), stored_grads.T, preferred_element_type=jnp.float32)
```

```python
import jax
import jax.numpy as jnp
from jax import lax
from jax.sharding import PartitionSpec as P

R = 32


def mod_perm(dz, dx, dc):
    pairs = []
    for m in range(16):
        z, x, c = m // 8, m // 2 % 4, m % 2
        pairs.append((m, (z + dz) % 2 * 8 + (x + dx) % 4 * 2 + (c + dc) % 2))
    return pairs


def store_perm(dz, dy):
    return [(s, (s // 4 + dz) % 2 * 4 + (s % 4 + dy) % 4) for s in range(8)]


def over_x(v, step):
    return lax.ppermute(v, "mod", mod_perm(0, step, 0))


def over_z_hi(v):
    return lax.ppermute(v, "mod", mod_perm(1, 0, 0))


def over_core(v):
    return lax.ppermute(v, "mod", mod_perm(0, 0, 1))


def over_y(v, step):
    return lax.ppermute(v, "store", store_perm(0, step))


def over_z_lo(v):
    return lax.ppermute(v, "store", store_perm(1, 0))


def pick(v, index, axis):
    return lax.dynamic_index_in_dim(v, index, axis, keepdims=False)


def gather_z_first(block):
    pair = jnp.stack([block, over_z_lo(block)])
    left = over_y(pair, 1)
    right = over_y(pair, -1)
    far = jnp.stack([over_y(left[0], 1), over_y(right[1], -1)])
    return jnp.stack([pair, left, far, right]).reshape(-1, block.shape[-1])


def gather_y_first(block):
    half = block.shape[0] // 2
    left = over_y(block, 1)
    right = over_y(block, -1)
    near = over_z_lo(jnp.stack([block, left, right]))
    far = jnp.concatenate([over_y(left[:half], 1), over_y(right[half:], -1)])
    far_z = over_z_lo(far)
    rows = [block, near[0], left, near[1], far, far_z, right, near[2]]
    return jnp.stack(rows).reshape(-1, block.shape[-1])


def add(*terms):
    total = terms[0].astype(jnp.float32)
    for term in terms[1:]:
        total = total + term.astype(jnp.float32)
    return total


def reduce_x(blocks, y, x):
    def block(step):
        return pick(blocks, (y - x - step) % 4, 0)

    half = blocks.shape[1] // 2
    to_next, to_prev, to_far, mine = block(1), block(-1), block(2), block(0)
    from_prev = over_x(jnp.stack([to_next[half:], to_far[:half]]), 1)
    from_next = over_x(jnp.stack([to_prev[:half], to_far[half:]]), -1)
    sum_prev = over_x(add(to_next[:half], from_prev[1]).astype(jnp.bfloat16), 1)
    sum_next = over_x(add(to_prev[half:], from_next[1]).astype(jnp.bfloat16), -1)
    low = add(mine[:half], from_next[0], sum_prev)
    high = add(mine[half:], from_prev[0], sum_next)
    return jnp.concatenate([low, high])


def scatter_x_first(part, y, x, z_mine):
    rows, width = part.shape[2], part.shape[3]
    reduced = reduce_x(part.reshape(4, 2 * rows, width), y, x).reshape(2, rows, width)
    received = over_z_hi(pick(reduced, 1 - z_mine, 0).astype(jnp.bfloat16))
    return add(pick(reduced, z_mine, 0), received)


def scatter_z_first(part, y, x, z_mine):
    received = over_z_hi(pick(part, 1 - z_mine, 1))
    both = add(pick(part, z_mine, 1), received).astype(jnp.bfloat16)
    return reduce_x(both, y, x)


def local(act_proj, grad_proj, token_mask, layer_of, layer_weight, fisher_inv, stored_grads):
    q_local, length, columns = act_proj.shape
    modules = columns // R
    place = lax.axis_index("mod")
    z_hi, x, core = place // 8, place // 2 % 4, place % 2
    owner = lax.axis_index("store")
    z_lo, y = owner // 4, owner % 4
    z_mine = (z_lo + z_hi) % 2
    valid_mask = token_mask.astype(jnp.bfloat16)[:, :, None]
    grad_side = (grad_proj * valid_mask).reshape(q_local, length, modules, R)
    act_side = act_proj.reshape(q_local, length, modules, R)
    per_sample = jnp.einsum(
        "qtmi,qtmj->qmij", grad_side, act_side, preferred_element_type=jnp.float32
    )
    per_sample = per_sample.reshape(q_local, modules, R * R).astype(jnp.bfloat16)
    picked = layer_of[:, None] == jnp.arange(layer_weight.shape[0], dtype=jnp.int32)[None, :]
    module_weight = jnp.sum(jnp.where(picked, layer_weight[None, :], 0.0), axis=1)
    grouped = lax.all_to_all(per_sample, "mod", split_axis=1, concat_axis=0, tiled=True)
    half = grouped.shape[0] // 2

    def conditioned(which):
        rows = lax.dynamic_slice_in_dim(grouped, which * half, half, 0)
        product = jnp.einsum("qkr,krc->qkc", rows, fisher_inv, preferred_element_type=jnp.float32)
        return (product * module_weight[None, :, None]).astype(jnp.bfloat16).reshape(half, -1)

    sibling_rows = gather_z_first(conditioned(1 - core))
    own_rows = gather_y_first(conditioned(core))
    width = stored_grads.shape[0] // 2
    outs = []
    for n, scatter in ((0, scatter_z_first), (1, scatter_x_first)):
        stored = stored_grads[n * width : (n + 1) * width]
        dims = (((1,), (1,)), ((), ()))
        for_sibling = lax.dot_general(sibling_rows, stored, dims, preferred_element_type=jnp.float32)
        from_sibling = over_core(for_sibling.astype(jnp.bfloat16))
        own = lax.dot_general(own_rows, stored, dims, preferred_element_type=jnp.float32)
        part = add(own, from_sibling).astype(jnp.bfloat16).reshape(4, 2, half, width)
        outs.append(scatter(part, y, x, z_mine))
    return jnp.concatenate(outs, axis=1)


def solution(mesh):
    in_specs = (
        P(("store", "mod"), None, None),
        P(("store", "mod"), None, None),
        P(("store", "mod"), None),
        P("mod"),
        P(),
        P("mod", None, None),
        P("store", "mod"),
    )
    out_specs = P("mod", "store")
    return jax.shard_map(local, mesh=mesh, in_specs=in_specs, out_specs=out_specs, check_vma=False)
```

```python
import jax
import jax.numpy as jnp
from jax import lax
from jax.experimental import pallas as pl
from jax.experimental.pallas import tpu as pltpu
from jax.sharding import PartitionSpec as P

R = 32


def mod_perm(dz, dx, dc):
    pairs = []
    for m in range(16):
        z, x, c = m // 8, m // 2 % 4, m % 2
        pairs.append((m, (z + dz) % 2 * 8 + (x + dx) % 4 * 2 + (c + dc) % 2))
    return pairs


def store_perm(dz, dy):
    return [(s, (s // 4 + dz) % 2 * 4 + (s % 4 + dy) % 4) for s in range(8)]


def over_x(v, step):
    return lax.ppermute(v, "mod", mod_perm(0, step, 0))


def over_z_hi(v):
    return lax.ppermute(v, "mod", mod_perm(1, 0, 0))


def over_core(v):
    return lax.ppermute(v, "mod", mod_perm(0, 0, 1))


def over_y(v, step):
    return lax.ppermute(v, "store", store_perm(0, step))


def over_z_lo(v):
    return lax.ppermute(v, "store", store_perm(1, 0))


def pick(v, index, axis):
    return lax.dynamic_index_in_dim(v, index, axis, keepdims=False)


def gather_z_first(block):
    pair = jnp.stack([block, over_z_lo(block)])
    left = over_y(pair, 1)
    right = over_y(pair, -1)
    far = jnp.stack([over_y(left[0], 1), over_y(right[1], -1)])
    return jnp.stack([pair, left, far, right]).reshape(-1, block.shape[-1])


def gather_y_first(block):
    half = block.shape[0] // 2
    left = over_y(block, 1)
    right = over_y(block, -1)
    near = over_z_lo(jnp.stack([block, left, right]))
    far = jnp.concatenate([over_y(left[:half], 1), over_y(right[half:], -1)])
    far_z = over_z_lo(far)
    rows = [block, near[0], left, near[1], far, far_z, right, near[2]]
    return jnp.stack(rows).reshape(-1, block.shape[-1])


def add(*terms):
    total = terms[0].astype(jnp.float32)
    for term in terms[1:]:
        total = total + term.astype(jnp.float32)
    return total


def reduce_x(blocks, y, x):
    def block(step):
        return pick(blocks, (y - x - step) % 4, 0)

    half = blocks.shape[1] // 2
    to_next, to_prev, to_far, mine = block(1), block(-1), block(2), block(0)
    from_prev = over_x(jnp.stack([to_next[half:], to_far[:half]]), 1)
    from_next = over_x(jnp.stack([to_prev[:half], to_far[half:]]), -1)
    sum_prev = over_x(add(to_next[:half], from_prev[1]).astype(jnp.bfloat16), 1)
    sum_next = over_x(add(to_prev[half:], from_next[1]).astype(jnp.bfloat16), -1)
    low = add(mine[:half], from_next[0], sum_prev)
    high = add(mine[half:], from_prev[0], sum_next)
    return jnp.concatenate([low, high])


def scatter_x_first(part, y, x, z_mine):
    rows, width = part.shape[2], part.shape[3]
    reduced = reduce_x(part.reshape(4, 2 * rows, width), y, x).reshape(2, rows, width)
    received = over_z_hi(pick(reduced, 1 - z_mine, 0).astype(jnp.bfloat16))
    return add(pick(reduced, z_mine, 0), received)


def scatter_z_first(part, y, x, z_mine):
    received = over_z_hi(pick(part, 1 - z_mine, 1))
    both = add(pick(part, z_mine, 1), received).astype(jnp.bfloat16)
    return reduce_x(both, y, x)


STEP = 4


def outer_kernel(mask_ref, grad_ref, act_ref, out_ref, diag_ref):
    module = lax.broadcasted_iota(jnp.int32, (R, 256), 1) // R
    slot = lax.broadcasted_iota(jnp.int32, (8, 128), 1) // R
    for q in range(STEP):
        mask = mask_ref[pl.ds(pl.program_id(0) * STEP + q, 1), :].astype(jnp.bfloat16)
        for group in range(4):
            columns = slice(group * 256, group * 256 + 256)
            grad_side = grad_ref[q, :, columns].T * mask
            full = jnp.dot(grad_side, act_ref[q, :, columns], preferred_element_type=jnp.float32)
            diag = full[:R]
            for m in range(1, 8):
                diag = jnp.where(module == m, full[m * R : m * R + R], diag)
            for tile in range(2):
                start = (q * 8 + 2 * group + tile) * R
                diag_ref[start : start + R, :] = diag[:, tile * 128 : tile * 128 + 128]
        for tile in range(8):
            start = (q * 8 + tile) * R
            rows = [diag_ref[pl.ds(start + p, 8, stride=4), :] for p in range(4)]
            packed = []
            for a in range(4):
                merged = None
                for p in range(4):
                    moved = rows[p] if p == a else pltpu.roll(rows[p], (p - a) % 4 * R, 1)
                    merged = moved if p == 0 else jnp.where(slot == p, moved, merged)
                packed.append(merged)
            for k in range(2):
                pair = jnp.concatenate(packed[2 * k : 2 * k + 2], axis=0)
                out_ref[2 * tile + k, q] = pair.astype(jnp.bfloat16)


def outer_products(token_mask, grad_proj, act_proj):
    queries, length, columns = grad_proj.shape
    return pl.pallas_call(
        outer_kernel,
        grid=(queries // STEP,),
        in_specs=[
            pl.BlockSpec((queries, length), lambda q: (0, 0)),
            pl.BlockSpec((STEP, length, columns), lambda q: (q, 0, 0)),
            pl.BlockSpec((STEP, length, columns), lambda q: (q, 0, 0)),
        ],
        out_specs=pl.BlockSpec((16, STEP, 16, 128), lambda q: (0, q, 0, 0)),
        out_shape=jax.ShapeDtypeStruct((16, queries, 16, 128), jnp.bfloat16),
        scratch_shapes=[pltpu.VMEM((STEP * 8 * R, 128), jnp.float32)],
    )(token_mask, grad_proj, act_proj)


def fisher_kernel(core_ref, weight_ref, rows_ref, fisher_ref, sibling_ref, own_ref, wide_ref):
    module = pl.program_id(0)

    @pl.when(module == 0)
    def _():
        wide_ref[...] = rows_ref[...].reshape(wide_ref.shape).astype(jnp.float32)

    count = wide_ref.shape[0] // 16
    pieces = [wide_ref[pl.ds(module * 8 + r, count, stride=16), :] for r in range(8)]
    left = jnp.concatenate(pieces, axis=1).astype(jnp.bfloat16)
    product = jnp.dot(left, fisher_ref[0], preferred_element_type=jnp.float32)
    scaled = (product * weight_ref[module]).astype(jnp.bfloat16)
    first = core_ref[0] == 0
    half = count // 2

    @pl.when(first)
    def _():
        own_ref[...] = scaled[:half]
        sibling_ref[...] = scaled[half:]

    @pl.when(jnp.logical_not(first))
    def _():
        own_ref[...] = scaled[half:]
        sibling_ref[...] = scaled[:half]


def conditioned_rows(core, module_weight, grouped, fisher_inv):
    sources, queries = grouped.shape[:2]
    modules, rank = fisher_inv.shape[:2]
    count = sources * queries
    out = jax.ShapeDtypeStruct((count // 2, modules * rank), jnp.bfloat16)
    out_spec = pl.BlockSpec((count // 2, rank), lambda m: (0, m))
    return pl.pallas_call(
        fisher_kernel,
        grid=(modules,),
        in_specs=[
            pl.BlockSpec(memory_space=pltpu.SMEM),
            pl.BlockSpec(memory_space=pltpu.SMEM),
            pl.BlockSpec(memory_space=pltpu.VMEM),
            pl.BlockSpec((1, rank, rank), lambda m: (m, 0, 0)),
        ],
        out_specs=[out_spec, out_spec],
        out_shape=[out, out],
        scratch_shapes=[pltpu.VMEM((count * 16, 128), jnp.float32)],
    )(core[None], module_weight, grouped, fisher_inv)


def compute(act_proj, grad_proj, token_mask, layer_of, layer_weight, fisher_inv, stored_grads):
    place = lax.axis_index("mod")
    z_hi, x, core = place // 8, place // 2 % 4, place % 2
    owner = lax.axis_index("store")
    z_lo, y = owner // 4, owner % 4
    z_mine = (z_lo + z_hi) % 2
    per_sample = outer_products(token_mask, grad_proj, act_proj)
    picked = layer_of[:, None] == jnp.arange(layer_weight.shape[0], dtype=jnp.int32)[None, :]
    module_weight = jnp.sum(jnp.where(picked, layer_weight[None, :], 0.0), axis=1)
    grouped = lax.all_to_all(per_sample, "mod", split_axis=0, concat_axis=0, tiled=True)
    sibling, mine = conditioned_rows(core, module_weight, grouped, fisher_inv)
    half = mine.shape[0]
    sibling_rows = gather_z_first(sibling)
    own_rows = gather_y_first(mine)
    dims = (((1,), (1,)), ((), ()))
    cut = stored_grads.shape[0] * 3 // 8
    stored = [stored_grads[:cut], stored_grads[cut:]]
    swapped = []
    for n in range(2):
        partial = lax.dot_general(sibling_rows, stored[n], dims, preferred_element_type=jnp.float32)
        partial = partial.astype(jnp.bfloat16)
        swapped.append(over_core(partial))
    outs = []
    for n, scatter in ((0, scatter_z_first), (1, scatter_x_first)):
        own = lax.dot_general(own_rows, stored[n], dims, preferred_element_type=jnp.float32)
        part = add(own, swapped[n]).astype(jnp.bfloat16).reshape(4, 2, half, -1)
        outs.append(scatter(part, y, x, z_mine))
    return jnp.concatenate(outs, axis=1)


def solution(mesh):
    in_specs = (
        P(("store", "mod"), None, None),
        P(("store", "mod"), None, None),
        P(("store", "mod"), None),
        P("mod"),
        P(),
        P("mod", None, None),
        P("store", "mod"),
    )
    out_specs = P("mod", "store")
    return jax.shard_map(compute, mesh=mesh, in_specs=in_specs, out_specs=out_specs, check_vma=False)
```

```python
import jax
import jax.numpy as jnp
from jax import lax
from jax.experimental import pallas as pl
from jax.experimental.pallas import tpu as pltpu
from jax.sharding import PartitionSpec as P

R = 32


def mod_perm(dz, dx, dc):
    pairs = []
    for m in range(16):
        z, x, c = m // 8, m // 2 % 4, m % 2
        pairs.append((m, (z + dz) % 2 * 8 + (x + dx) % 4 * 2 + (c + dc) % 2))
    return pairs


def store_perm(dz, dy):
    return [(s, (s // 4 + dz) % 2 * 4 + (s % 4 + dy) % 4) for s in range(8)]


def over_x(v, step):
    return lax.ppermute(v, "mod", mod_perm(0, step, 0))


def over_z_hi(v):
    return lax.ppermute(v, "mod", mod_perm(1, 0, 0))


def over_core(v):
    return lax.ppermute(v, "mod", mod_perm(0, 0, 1))


def over_y(v, step):
    return lax.ppermute(v, "store", store_perm(0, step))


def over_z_lo(v):
    return lax.ppermute(v, "store", store_perm(1, 0))


def pick(v, index, axis):
    return lax.dynamic_index_in_dim(v, index, axis, keepdims=False)


def gather_z_first(block):
    pair = jnp.stack([block, over_z_lo(block)])
    left = over_y(pair, 1)
    right = over_y(pair, -1)
    far = jnp.stack([over_y(left[0], 1), over_y(right[1], -1)])
    return jnp.stack([pair, left, far, right]).reshape(-1, block.shape[-1])


def gather_y_first(block):
    half = block.shape[0] // 2
    left = over_y(block, 1)
    right = over_y(block, -1)
    near = over_z_lo(jnp.stack([block, left, right]))
    far = jnp.concatenate([over_y(left[:half], 1), over_y(right[half:], -1)])
    far_z = over_z_lo(far)
    rows = [block, near[0], left, near[1], far, far_z, right, near[2]]
    return jnp.stack(rows).reshape(-1, block.shape[-1])


def add(*terms):
    total = terms[0].astype(jnp.float32)
    for term in terms[1:]:
        total = total + term.astype(jnp.float32)
    return total


def reduce_x(blocks, y, x):
    def block(step):
        return pick(blocks, (y - x - step) % 4, 0)

    half = blocks.shape[1] // 2
    to_next, to_prev, to_far, mine = block(1), block(-1), block(2), block(0)
    from_prev = over_x(jnp.stack([to_next[half:], to_far[:half]]), 1)
    from_next = over_x(jnp.stack([to_prev[:half], to_far[half:]]), -1)
    sum_prev = over_x(add(to_next[:half], from_prev[1]).astype(jnp.bfloat16), 1)
    sum_next = over_x(add(to_prev[half:], from_next[1]).astype(jnp.bfloat16), -1)
    low = add(mine[:half], from_next[0], sum_prev)
    high = add(mine[half:], from_prev[0], sum_next)
    return jnp.concatenate([low, high])


def scatter_x_first(part, y, x, z_mine):
    rows, width = part.shape[2], part.shape[3]
    reduced = reduce_x(part.reshape(4, 2 * rows, width), y, x).reshape(2, rows, width)
    received = over_z_hi(pick(reduced, 1 - z_mine, 0).astype(jnp.bfloat16))
    return add(pick(reduced, z_mine, 0), received)


def scatter_z_first(part, y, x, z_mine):
    received = over_z_hi(pick(part, 1 - z_mine, 1))
    both = add(pick(part, z_mine, 1), received).astype(jnp.bfloat16)
    return reduce_x(both, y, x)


STEP = 4


def outer_kernel(mask_ref, grad_ref, act_ref, out_ref, diag_ref):
    module = lax.broadcasted_iota(jnp.int32, (R, 256), 1) // R
    slot = lax.broadcasted_iota(jnp.int32, (8, 128), 1) // R
    for q in range(STEP):
        mask = mask_ref[pl.ds(pl.program_id(0) * STEP + q, 1), :].astype(jnp.bfloat16)
        for group in range(4):
            columns = slice(group * 256, group * 256 + 256)
            grad_side = grad_ref[q, :, columns].T * mask
            full = jnp.dot(grad_side, act_ref[q, :, columns], preferred_element_type=jnp.float32)
            diag = full[:R]
            for m in range(1, 8):
                diag = jnp.where(module == m, full[m * R : m * R + R], diag)
            for tile in range(2):
                start = (q * 8 + 2 * group + tile) * R
                diag_ref[start : start + R, :] = diag[:, tile * 128 : tile * 128 + 128]
        for tile in range(8):
            start = (q * 8 + tile) * R
            rows = [diag_ref[pl.ds(start + p, 8, stride=4), :] for p in range(4)]
            packed = []
            for a in range(4):
                merged = None
                for p in range(4):
                    moved = rows[p] if p == a else pltpu.roll(rows[p], (p - a) % 4 * R, 1)
                    merged = moved if p == 0 else jnp.where(slot == p, moved, merged)
                packed.append(merged)
            for k in range(2):
                pair = jnp.concatenate(packed[2 * k : 2 * k + 2], axis=0)
                out_ref[2 * tile + k, q] = pair.astype(jnp.bfloat16)


def outer_products(token_mask, grad_proj, act_proj):
    queries, length, columns = grad_proj.shape
    return pl.pallas_call(
        outer_kernel,
        grid=(queries // STEP,),
        in_specs=[
            pl.BlockSpec((queries, length), lambda q: (0, 0)),
            pl.BlockSpec((STEP, length, columns), lambda q: (q, 0, 0)),
            pl.BlockSpec((STEP, length, columns), lambda q: (q, 0, 0)),
        ],
        out_specs=pl.BlockSpec((16, STEP, 16, 128), lambda q: (0, q, 0, 0)),
        out_shape=jax.ShapeDtypeStruct((16, queries, 16, 128), jnp.bfloat16),
        scratch_shapes=[pltpu.VMEM((STEP * 8 * R, 128), jnp.float32)],
    )(token_mask, grad_proj, act_proj)


def fisher_kernel(core_ref, weight_ref, rows_ref, fisher_ref, sibling_ref, own_ref, wide_ref, near_ref, semaphores):
    modules = fisher_ref.shape[0]
    copies = [pltpu.make_async_copy(fisher_ref.at[m], near_ref.at[m], semaphores.at[m]) for m in range(modules)]
    for copy in copies:
        copy.start()
    wide_ref[...] = rows_ref[...].reshape(wide_ref.shape).astype(jnp.float32)
    count = wide_ref.shape[0] // 16
    half = count // 2
    first = core_ref[0] == 0
    rank = fisher_ref.shape[1]
    for m in range(modules):
        pieces = [wide_ref[pl.ds(m * 8 + r, count, stride=16), :] for r in range(8)]
        left = jnp.concatenate(pieces, axis=1).astype(jnp.bfloat16)
        copies[m].wait()
        product = jnp.dot(left, near_ref[m], preferred_element_type=jnp.float32)
        scaled = (product * weight_ref[m]).astype(jnp.bfloat16)
        columns = slice(m * rank, m * rank + rank)
        own_ref[:, columns] = jnp.where(first, scaled[:half], scaled[half:])
        sibling_ref[:, columns] = jnp.where(first, scaled[half:], scaled[:half])


def conditioned_rows(core, module_weight, grouped, fisher_inv):
    sources, queries = grouped.shape[:2]
    modules, rank = fisher_inv.shape[:2]
    count = sources * queries
    out = jax.ShapeDtypeStruct((count // 2, modules * rank), jnp.bfloat16)
    near = pl.BlockSpec(memory_space=pltpu.VMEM)
    scalars = pl.BlockSpec(memory_space=pltpu.SMEM)
    return pl.pallas_call(
        fisher_kernel,
        in_specs=[scalars, scalars, near, pl.BlockSpec(memory_space=pl.ANY)],
        out_specs=[near, near],
        out_shape=[out, out],
        scratch_shapes=[
            pltpu.VMEM((count * 16, 128), jnp.float32),
            pltpu.VMEM(fisher_inv.shape, jnp.bfloat16),
            pltpu.SemaphoreType.DMA((modules,)),
        ],
    )(core[None], module_weight, grouped, fisher_inv)


def compute(act_proj, grad_proj, token_mask, layer_of, layer_weight, fisher_inv, stored_grads):
    place = lax.axis_index("mod")
    z_hi, x, core = place // 8, place // 2 % 4, place % 2
    owner = lax.axis_index("store")
    z_lo, y = owner // 4, owner % 4
    z_mine = (z_lo + z_hi) % 2
    per_sample = outer_products(token_mask, grad_proj, act_proj)
    picked = layer_of[:, None] == jnp.arange(layer_weight.shape[0], dtype=jnp.int32)[None, :]
    module_weight = jnp.sum(jnp.where(picked, layer_weight[None, :], 0.0), axis=1)
    grouped = lax.all_to_all(per_sample, "mod", split_axis=0, concat_axis=0, tiled=True)
    sibling, mine = conditioned_rows(core, module_weight, grouped, fisher_inv)
    half = mine.shape[0]
    sibling_rows = gather_z_first(sibling)
    own_rows = gather_y_first(mine)
    dims = (((1,), (1,)), ((), ()))
    cut = stored_grads.shape[0] * 3 // 8
    stored = [stored_grads[:cut], stored_grads[cut:]]
    swapped = []
    for n in range(2):
        partial = lax.dot_general(sibling_rows, stored[n], dims, preferred_element_type=jnp.float32)
        partial = partial.astype(jnp.bfloat16)
        swapped.append(over_core(partial))
    outs = []
    for n, scatter in ((0, scatter_z_first), (1, scatter_x_first)):
        own = lax.dot_general(own_rows, stored[n], dims, preferred_element_type=jnp.float32)
        part = add(own, swapped[n]).astype(jnp.bfloat16).reshape(4, 2, half, -1)
        outs.append(scatter(part, y, x, z_mine))
    return jnp.concatenate(outs, axis=1)


def solution(mesh):
    in_specs = (
        P(("store", "mod"), None, None),
        P(("store", "mod"), None, None),
        P(("store", "mod"), None),
        P("mod"),
        P(),
        P("mod", None, None),
        P("store", "mod"),
    )
    out_specs = P("mod", "store")
    return jax.shard_map(compute, mesh=mesh, in_specs=in_specs, out_specs=out_specs, check_vma=False)
```
